256 devices in a mesh: wide: 64 (over y, z, core), narrow: 4 (over x).
Axes of the slice: x: 4, y: 4, z: 8, core: 2. Of those that a mesh axis runs over, the one named last changes fastest.
Arguments:
- embedding: float32 [131072, 128], P(('wide', 'narrow'))
- tile_blocks: bfloat16 [64, 4, 22, 512, 512], P('wide', 'narrow'), may hold values from -0.125 to 0.125
- tile_row: int32 [64, 4, 22], P('wide', 'narrow'), may hold values from 0 to 3
- tile_col: int32 [64, 4, 22], P('wide', 'narrow'), may hold values from 0 to 63
- counts: int32 [64, 4], P('wide', 'narrow'), may hold values from 1 to 22, as said below
Outputs:
- orthonormal: float32 [131072, 128], P(('wide', 'narrow'))
The draws below stay inside these ranges and needn't reach their ends.
Inputs may be any that keep to these rules, and one draw needn't show every extreme that they name: Slots 0 to counts[w, n] - 1 of device (w, n) hold its tiles, the others are unused; some device has all 22 slots live.
All inputs are finite; a program needn't handle non-finite values.
Results may differ from the reference program's by a relative error of at most 0.0036.
Values may be sent and summed in bfloat16 or wider, within the bound.
No kernel may reach another device: no remote copies, remote signals or barrier semaphores. Data moves between devices by JAX's collectives and lax.ppermute only.
A program may use at most 64 MiB of HBM per device.

```python
import math
import jax
import jax.numpy as jnp
from jax import lax

TILE = 512
EMB = 128
TILE_ROWS = 1
SLOTS = 22
WIDE_DEVS = 64
NARROW_DEVS = 4
SLAB_TILES = 4
GROUP_TILES = 64
NODES = 131072
N_WIDE = 64
N_NARROW = 4


def draw_embedding(key, part):
    keys = jax.random.split(jax.random.fold_in(key, 11), 3)
    row_pos = jnp.arange(NODES, dtype=jnp.float32)[:, None] / NODES
    row_scale = jnp.exp(math.log(3.0) * row_pos) * jnp.exp(jax.random.uniform(keys[1], (NODES, 1), jnp.float32, -math.log(2.0), math.log(2.0)))
    col_scale = jnp.exp(jax.random.uniform(keys[2], (1, EMB), jnp.float32, 0.0, math.log(10.0)))
    base = jax.random.normal(keys[0], (NODES, EMB), jnp.float32)
    return base * row_scale * col_scale / 4.0


def draw_counts(key, part):
    keys = jax.random.split(jax.random.fold_in(key, 23), 2)
    drawn = jax.random.randint(keys[0], (WIDE_DEVS, NARROW_DEVS), 0, SLOTS, jnp.int32)
    filled = 1 + drawn * (drawn + SLOTS) // (2 * SLOTS)
    flat_counts = filled.reshape(-1)
    position = jax.random.randint(keys[1], (), 0, WIDE_DEVS * NARROW_DEVS, jnp.int32)
    flat_counts = flat_counts.at[position].set(SLOTS)
    return flat_counts.reshape(WIDE_DEVS, NARROW_DEVS).astype(jnp.int32)


def plant(array, own_key, smallest, largest):
    extent = array.shape
    place = [jax.random.randint(jax.random.fold_in(own_key, axis), (), 0, extent[axis]) for axis in range(len(extent))]
    array = array.at[tuple(place)].set(smallest)
    longest = extent.index(max(extent))
    place[longest] = (place[longest] + 1) % extent[longest]
    return array.at[tuple(place)].set(largest)


def level_of(rng, shape, cuts, least, largest):
    gain = 1.0
    for dim, shards_of in cuts:
        draws = jax.random.uniform(jax.random.fold_in(jax.random.fold_in(rng, 6), dim), (shards_of,), jnp.float32, least / len(cuts), largest / len(cuts))
        gain = gain * jnp.repeat(jnp.exp(draws), shape[dim] // shards_of).reshape((-1,) + (1,) * (len(shape) - 1 - dim))
    return gain


def normal_values(own_key, dims, deviation, bound, cuts=(), kind=jnp.bfloat16):
    gain = level_of(own_key, dims, cuts, -0.22, 0.18) if cuts else 1.0
    values = jax.random.normal(own_key, dims, jnp.float32) * deviation * gain
    return jnp.minimum(jnp.maximum(values, -bound), bound).astype(kind)


def setup_inputs(seed: int = 0) -> dict:
    key_of = jax.random.split(jax.random.key(seed), 6)
    embedding = draw_embedding(jax.random.fold_in(key_of[5], 71), 0)
    tile_blocks = normal_values(key_of[1], (WIDE_DEVS, NARROW_DEVS, SLOTS, TILE, TILE), (4 * TILE) ** -0.5, 0.125, ((0, 64), (1, 4)))
    tile_row = plant(jax.random.randint(key_of[2], (WIDE_DEVS, NARROW_DEVS, SLOTS), 0, SLAB_TILES), jax.random.fold_in(key_of[2], 1), 0, SLAB_TILES - 1).astype(jnp.int32)
    tile_col = plant(jax.random.randint(key_of[3], (WIDE_DEVS, NARROW_DEVS, SLOTS), 0, GROUP_TILES), jax.random.fold_in(key_of[3], 1), 0, GROUP_TILES - 1).astype(jnp.int32)
    counts = draw_counts(jax.random.fold_in(key_of[5], 71), 0)
    return dict(embedding=embedding, tile_blocks=tile_blocks, tile_row=tile_row, tile_col=tile_col, counts=counts)


def apply_operator(values_bf, tile_blocks, tile_row, tile_col, counts):
    blocks = values_bf.reshape(NODES // TILE, TILE, EMB)

    def add_tile(carry, flat_index):
        wide_pos = flat_index // (N_NARROW * SLOTS)
        narrow_pos = flat_index // SLOTS % N_NARROW
        slot = flat_index % SLOTS
        column = tile_col[wide_pos, narrow_pos, slot]
        global_col = (column // TILE_ROWS * N_NARROW + narrow_pos) * TILE_ROWS + column % TILE_ROWS
        global_row = wide_pos * N_NARROW * TILE_ROWS + tile_row[wide_pos, narrow_pos, slot]

        def compute(accum):
            product = jnp.dot(tile_blocks[wide_pos, narrow_pos, slot].astype(jnp.float32), blocks[global_col].astype(jnp.float32), preferred_element_type=jnp.float32)
            return accum.at[global_row].add(product)

        def keep(accum):
            return accum
        carry = lax.cond(slot < counts[wide_pos, narrow_pos], compute, keep, carry)
        return (carry, None)
    start = jnp.zeros((NODES // TILE, TILE, EMB), jnp.float32)
    result, unused = lax.scan(add_tile, start, jnp.arange(N_WIDE * N_NARROW * SLOTS, dtype=jnp.int32))
    return result.reshape(NODES, EMB)

def reference(embedding, tile_blocks, tile_row, tile_col, counts):
    emb_bf = embedding.astype(jnp.bfloat16)
    first_order = apply_operator(emb_bf, tile_blocks, tile_row, tile_col, counts)
    first_bf = first_order.astype(jnp.bfloat16)
    second = 2.0 * apply_operator(first_bf, tile_blocks, tile_row, tile_col, counts) - embedding
    spectral = 1.2661 * embedding - 1.1303 * first_order + 0.2715 * second
    gram_matrix = lax.dot_general(spectral, spectral, (((0,), (0,)), ((), ())), precision=lax.Precision.HIGHEST)
    lower_factor = jnp.linalg.cholesky(gram_matrix)
    solved = jax.scipy.linalg.solve_triangular(lower_factor, spectral.T, lower=True)
    return solved.T * jnp.sqrt(jnp.float32(NODES))
```

```python
import functools

import jax
import jax.numpy as jnp
import numpy as np
from jax import lax
from jax.experimental import pallas as pl
from jax.experimental.pallas import tpu as pltpu
from jax.sharding import Mesh, PartitionSpec as P

NY, NZ, NC, NX = 4, 8, 2, 4
PLANE = ("y", "z", "c")
PIECES = 10


def plane_index(y, z, c):
    return ((y % NY) * NZ + z % NZ) * NC + c


def step_pairs(hop):
    first = []
    for y in range(NY):
        for z in range(NZ):
            first.append((plane_index(y, z, 0), plane_index(y, z + hop, 0)))
            first.append((plane_index(y, z, 1), plane_index(y + hop, z, 1)))
    return first


def bundle_pairs(hop):
    second = []
    for y in range(NY):
        for z in range(NZ):
            second.append((plane_index(y, z, 0), plane_index(y + hop, z, 0)))
            second.append((plane_index(y, z, 1), plane_index(y, z + hop, 1)))
    return second


def axis_shift(value, axis, hop):
    n = lax.axis_size(axis)
    return lax.ppermute(value, axis, [(i, (i + hop) % n) for i in range(n)])


def axis_swap(value, axis, bit):
    n = lax.axis_size(axis)
    return lax.ppermute(value, axis, [(i, i ^ bit) for i in range(n)])


def stack_blocks(parts):
    which = lax.broadcasted_iota(jnp.int32, (len(parts), 1, 1), 0)
    shape = (len(parts),) + parts[0].shape
    out = jnp.broadcast_to(parts[-1][None], shape)
    for i in range(len(parts) - 2, -1, -1):
        out = jnp.where(which == i, parts[i][None], out)
    return out


def gather_blocks(block, core):
    plus1, minus1 = step_pairs(1), step_pairs(-1)
    plus2, minus2 = step_pairs(2), step_pairs(-2)
    s = lambda v, pairs: lax.ppermute(v, PLANE, pairs)
    swap = lambda v: axis_shift(v, "c", 1)
    r1p, r1m = s(block, plus1), s(block, minus1)
    r2p, r2m = s(block, plus2), s(block, minus2)
    bplus, bminus = bundle_pairs(1), bundle_pairs(-1)
    lo = stack_blocks([block, r1p, r1m, r2p])
    g1p, g1m = s(lo, bplus), s(lo, bminus)
    r3p, r3m = s(r2p, plus1), s(r2m, minus1)
    r4p = s(r2p, plus2)
    hi = stack_blocks([r2m, r3p, r3m, r4p])
    zero = core == 0
    g2p = s(g1p, bplus)
    g2m = s(jnp.where(zero, hi, g1m), bminus)
    g3p = s(jnp.where(zero, hi, g2p), bplus)
    g3m = s(g2m, bminus)
    g4p = s(g3p[:2], bplus)
    g4m = s(g3m[2:], bminus)
    mine = [lo, hi, g1p, g1m, g2p, g2m, g3p, g3m, g4p, g4m]
    return mine + [swap(v) for v in mine]


def piece_table():
    table = np.zeros((NC, NY, NZ), np.int32)
    lo_z, hi_z = [0, -1, 1, -2], [2, -3, 3, -4]
    for off in range(4):
        for piece, dy, offsets in (
            (0, 0, lo_z), (1, 0, hi_z), (2, -1, lo_z), (3, 1, lo_z),
            (4, -2, lo_z), (5, 1, hi_z), (6, -1, hi_z), (7, 2, hi_z),
        ):
            table[0, dy % NY, offsets[off] % NZ] = piece * 4 + off
    col_y = [0, -1, 1, -2]
    for off in range(4):
        for piece, dz in ((0, 0), (2, -1), (3, 1), (4, -2), (5, 2), (6, -3), (7, 3)):
            table[1, col_y[off] % NY, dz % NZ] = piece * 4 + off
        table[1, col_y[off] % NY, 4] = (8 + off // 2) * 4 + off % 2
    return table.reshape(-1)


def tile_kernel(slots, meta, tiles, *refs):
    pieces = refs[: 2 * PIECES]
    own_ref, one_ref, two_ref, three_ref = refs[2 * PIECES : 2 * PIECES + 4]
    tile_buf, block_buf, acc, tile_sem, block_sem = refs[2 * PIECES + 4 :]
    live = meta[2 * slots]

    def start(s, carry):
        pltpu.make_async_copy(tiles.at[s], tile_buf.at[s], tile_sem.at[s]).start()
        place = meta[s]
        piece = place // 4
        off = place % 4
        for i in range(2 * PIECES):

            @pl.when(piece == i)
            def _():
                inner = jnp.minimum(off, pieces[i].shape[0] - 1)
                pltpu.make_async_copy(pieces[i].at[inner], block_buf.at[s], block_sem.at[s]).start()

        return carry

    lax.fori_loop(0, live, start, 0)
    acc[...] = jnp.zeros_like(acc)

    def work(s, carry):
        pltpu.make_async_copy(tiles.at[s], tile_buf.at[s], tile_sem.at[s]).wait()
        pltpu.make_async_copy(pieces[0].at[0], block_buf.at[s], block_sem.at[s]).wait()
        row = meta[slots + s]
        acc[row] += jnp.dot(tile_buf[s], block_buf[s], preferred_element_type=jnp.float32)
        return carry

    lax.fori_loop(0, live, work, 0)
    own_ref[...] = acc[0]
    one_ref[...] = acc[1].astype(jnp.bfloat16)
    two_ref[...] = acc[2].astype(jnp.bfloat16)
    three_ref[...] = acc[3].astype(jnp.bfloat16)


def apply_operator(block, tiles, meta, core):
    slots, tile, _ = tiles.shape
    width = block.shape[1]
    pieces = gather_blocks(block, core)
    anyspec = pl.BlockSpec(memory_space=pl.ANY)
    vmem = pl.BlockSpec(memory_space=pltpu.VMEM)
    shape = lambda t: jax.ShapeDtypeStruct((tile, width), t)
    own, one, two, three = pl.pallas_call(
        functools.partial(tile_kernel, slots),
        out_shape=[shape(jnp.float32)] + [shape(jnp.bfloat16)] * 3,
        in_specs=[pl.BlockSpec(memory_space=pltpu.SMEM)] + [anyspec] * (1 + 2 * PIECES),
        out_specs=[vmem] * 4,
        scratch_shapes=[
            pltpu.VMEM((slots, tile, tile), jnp.bfloat16),
            pltpu.VMEM((slots, tile, width), jnp.bfloat16),
            pltpu.VMEM((NX, tile, width), jnp.float32),
            pltpu.SemaphoreType.DMA((slots,)),
            pltpu.SemaphoreType.DMA((slots,)),
        ],
        compiler_params=pltpu.CompilerParams(vmem_limit_bytes=24 << 20),
        cost_estimate=pl.CostEstimate(
            flops=2 * slots * tile * tile * width, bytes_accessed=slots * tile * (tile + width) * 2, transcendentals=0
        ),
        name="tile_products",
    )(meta, tiles, *pieces)
    f32 = jnp.float32
    return (
        own
        + axis_shift(one, "x", 1).astype(f32)
        + axis_shift(two, "x", 2).astype(f32)
        + axis_shift(three, "x", 3).astype(f32)
    )


def local(embedding, tile_blocks, tile_row, tile_col, counts):
    tiles = tile_blocks.reshape(tile_blocks.shape[-3:])
    slots = tiles.shape[0]
    y, z, core, x = (lax.axis_index(a) for a in ("y", "z", "c", "x"))
    col = tile_col.reshape(slots)
    from_y, from_z, from_c = col // (NZ * NC), col // NC % NZ, col % NC
    dy, dz = (from_y - y) % NY, (from_z - z) % NZ
    place = jnp.take(jnp.asarray(piece_table()), (from_c * NY + dy) * NZ + dz, axis=0)
    place = place + jnp.where(from_c == core, 0, PIECES * 4)
    row = (tile_row.reshape(slots) - x) % NX
    meta = jnp.concatenate([place, row, counts.reshape(1)]).astype(jnp.int32)

    emb_bf = embedding.astype(jnp.bfloat16)
    first_order = apply_operator(emb_bf, tiles, meta, core)
    first_bf = first_order.astype(jnp.bfloat16)
    second = 2.0 * apply_operator(first_bf, tiles, meta, core) - embedding
    spectral = 1.2661 * embedding - 1.1303 * first_order + 0.2715 * second
    gram = lax.dot_general(
        spectral, spectral, (((0,), (0,)), ((), ())), precision=lax.Precision.HIGHEST
    )
    gram = gram + axis_swap(gram, "c", 1)
    for axis in ("x", "y"):
        gram = gram + axis_shift(gram, axis, 1) + axis_shift(gram, axis, 2) + axis_shift(gram, axis, 3)
    for bit in (1, 2, 4):
        gram = gram + axis_swap(gram, "z", bit)
    lower_factor = jnp.linalg.cholesky(gram)
    solved = jax.scipy.linalg.solve_triangular(lower_factor, spectral.T, lower=True)
    node_total = embedding.shape[0] * NY * NZ * NC * NX
    return solved.T * jnp.sqrt(jnp.float32(node_total))


def solution(mesh):
    fine = Mesh(mesh.devices.reshape(NY, NZ, NC, NX), ("y", "z", "c", "x"))
    wide = ("y", "z", "c")
    placed = (
        P(("y", "z", "c", "x"), None),
        P(wide, "x", None, None, None),
        P(wide, "x", None),
        P(wide, "x", None),
        P(wide, "x"),
    )
    return jax.shard_map(
        local, mesh=fine, in_specs=placed, out_specs=P(("y", "z", "c", "x"), None), check_vma=False
    )
```

```python
import functools

import jax
import jax.numpy as jnp
import numpy as np
from jax import lax
from jax.experimental import pallas as pl
from jax.experimental.pallas import tpu as pltpu
from jax.sharding import Mesh, PartitionSpec as P

NY, NZ, NC, NX = 4, 8, 2, 4
PLANE = ("y", "z", "c")


def plane_index(y, z, c):
    return ((y % NY) * NZ + z % NZ) * NC + c


def step_pairs(hop):
    first = []
    for y in range(NY):
        for z in range(NZ):
            first.append((plane_index(y, z, 0), plane_index(y, z + hop, 0)))
            first.append((plane_index(y, z, 1), plane_index(y + hop, z, 1)))
    return first


def bundle_pairs(hop):
    second = []
    for y in range(NY):
        for z in range(NZ):
            second.append((plane_index(y, z, 0), plane_index(y + hop, z, 0)))
            second.append((plane_index(y, z, 1), plane_index(y, z + hop, 1)))
    return second


def axis_shift(value, axis, hop):
    n = lax.axis_size(axis)
    return lax.ppermute(value, axis, [(i, (i + hop) % n) for i in range(n)])


def axis_swap(value, axis, bit):
    n = lax.axis_size(axis)
    return lax.ppermute(value, axis, [(i, i ^ bit) for i in range(n)])


def stack_blocks(parts):
    which = lax.broadcasted_iota(jnp.int32, (len(parts), 1, 1), 0)
    shape = (len(parts),) + parts[0].shape
    out = jnp.broadcast_to(parts[-1][None], shape)
    for i in range(len(parts) - 2, -1, -1):
        out = jnp.where(which == i, parts[i][None], out)
    return out


def far_pairs():
    pairs = []
    for y in range(NY):
        for z in range(NZ):
            pairs.append((plane_index(y, z, 0), plane_index(y, z - 2, 0)))
            pairs.append((plane_index(y, z, 1), plane_index(y, z + 4, 1)))
    return pairs


def send(value, pairs):
    return lax.ppermute(value, PLANE, pairs)


def swap(value):
    return axis_shift(value, "c", 1)


def gather_blocks(block, core):
    zero = core == 0
    plus1, minus1, plus2 = step_pairs(1), step_pairs(-1), step_pairs(2)
    bplus, bminus = bundle_pairs(1), bundle_pairs(-1)
    a1 = send(block, plus1)
    a2 = send(block, minus1)
    a3 = send(block, plus2)
    a4 = send(block, far_pairs())
    lo = stack_blocks([block, a1, a2, a3])
    g1p = send(lo, bplus)
    g1m = send(lo, bminus)
    onward = jnp.where(zero, a3, a4)
    a5 = send(onward, plus1)
    a6 = send(a4, minus1)
    a7 = send(onward, plus2)
    hi = stack_blocks([a4, a5, a6, a7])
    g2p = send(g1p, bplus)
    g2m = send(jnp.where(zero, hi, g1m), bminus)
    g3p = send(jnp.where(zero, hi, g2p), bplus)
    g3m = send(g2m, bminus)
    mine = [lo, hi, g1p, g1m, g2p, g2m, g3p, g3m]
    theirs = [swap(v) for v in mine]
    return mine + theirs


def place_table():
    table = np.zeros((NC, NY, NZ), np.int32)
    lo_z, hi_z, col_y = [0, -1, 1, -2], [2, -3, 3, -4], [0, -1, 1, -2]
    rows = ((0, 0, lo_z), (1, 0, hi_z), (2, -1, lo_z), (3, 1, lo_z), (4, -2, lo_z), (5, 1, hi_z), (6, -1, hi_z), (7, 2, hi_z))
    columns = ((0, 0), (1, 4), (2, -1), (3, 1), (4, -2), (5, 2), (6, -3), (7, 3))
    for off in range(4):
        for piece, dy, offsets in rows:
            table[0, dy % NY, offsets[off] % NZ] = piece * 4 + off
        for piece, dz in columns:
            table[1, col_y[off] % NY, dz % NZ] = piece * 4 + off
    assert all(sorted(t.reshape(-1)) == list(range(NY * NZ)) for t in table)
    return table.reshape(-1)


def tile_kernel(slots, meta, tiles, *refs):
    *pieces, own_ref, one_ref, two_ref, three_ref, acc, picked = refs
    span = pieces[0].shape[0]
    live = meta[2 * slots]
    acc[...] = jnp.zeros_like(acc)

    def work(pair, carry):
        both = (2 * pair, 2 * pair + 1)
        for i, s in enumerate(both):
            place = meta[s]
            for p, piece in enumerate(pieces):

                @pl.when(place // span == p)
                def _():
                    picked[i] = piece[place % span]

        products = [
            jnp.dot(tiles[s], picked[i], preferred_element_type=jnp.float32) for i, s in enumerate(both)
        ]
        for i, s in enumerate(both):
            row = jnp.where(s < live, meta[slots + s], NX)
            acc[row] += products[i]
        return carry

    lax.fori_loop(0, (live + 1) // 2, work, 0)
    own_ref[...] = acc[0]
    one_ref[...] = acc[1].astype(jnp.bfloat16)
    two_ref[...] = acc[2].astype(jnp.bfloat16)
    three_ref[...] = acc[3].astype(jnp.bfloat16)


def apply_operator(block, tiles, meta, core):
    slots, tile, _ = tiles.shape
    assert slots % 2 == 0
    width = block.shape[1]
    pieces = gather_blocks(block, core)
    vmem = pl.BlockSpec(memory_space=pltpu.VMEM)
    shape = lambda t: jax.ShapeDtypeStruct((tile, width), t)
    own, one, two, three = pl.pallas_call(
        functools.partial(tile_kernel, slots),
        out_shape=[shape(jnp.float32)] + [shape(jnp.bfloat16)] * 3,
        in_specs=[pl.BlockSpec(memory_space=pltpu.SMEM), vmem] + [vmem] * len(pieces),
        out_specs=[vmem] * 4,
        scratch_shapes=[
            pltpu.VMEM((NX + 1, tile, width), jnp.float32),
            pltpu.VMEM((2, tile, width), jnp.bfloat16),
        ],
        compiler_params=pltpu.CompilerParams(vmem_limit_bytes=24 << 20),
        cost_estimate=pl.CostEstimate(
            flops=2 * slots * tile * tile * width, bytes_accessed=slots * tile * (tile + width) * 2, transcendentals=0
        ),
        name="tile_products",
    )(meta, tiles, *pieces)
    f32 = jnp.float32
    one = axis_shift(one, "x", 1)
    three = axis_shift(three, "x", 3)
    two = axis_shift(two, "x", 2)
    return own + one.astype(f32) + three.astype(f32) + two.astype(f32)


def sum_over_devices(gram, core):
    half = gram.shape[0] // 2
    zero = core == 0
    top, bottom = gram[:half], gram[half:]
    part = jnp.where(zero, top, bottom) + axis_shift(jnp.where(zero, bottom, top), "c", 1)
    for axis in ("x", "y"):
        part = part + axis_shift(part, axis, 1) + axis_shift(part, axis, 3) + axis_shift(part, axis, 2)
    part = part + axis_shift(part, "z", 2) + axis_shift(part, "z", 6) + axis_shift(part, "z", 4)
    part = part + axis_swap(part, "z", 1)
    other = axis_shift(part, "c", 1)
    return jnp.concatenate([jnp.where(zero, part, other), jnp.where(zero, other, part)], axis=0)


def local(embedding, tile_blocks, tile_row, tile_col, counts):
    tiles = tile_blocks.reshape(tile_blocks.shape[-3:])
    slots = tiles.shape[0]
    y, z, core, x = (lax.axis_index(a) for a in ("y", "z", "c", "x"))
    col = tile_col.reshape(slots)
    from_y, from_z, from_c = col // (NZ * NC), col // NC % NZ, col % NC
    dy, dz = (from_y - y) % NY, (from_z - z) % NZ
    place = jnp.take(jnp.asarray(place_table()), (from_c * NY + dy) * NZ + dz, axis=0)
    place = place + jnp.where(from_c == core, 0, NY * NZ)
    row = (tile_row.reshape(slots) - x) % NX
    meta = jnp.concatenate([place, row, counts.reshape(1)]).astype(jnp.int32)

    emb_bf = embedding.astype(jnp.bfloat16)
    first_order = apply_operator(emb_bf, tiles, meta, core)
    first_bf = first_order.astype(jnp.bfloat16)
    applied = apply_operator(first_bf, tiles, meta, core)
    second = 2.0 * applied - embedding
    spectral = 1.2661 * embedding - 1.1303 * first_order + 0.2715 * second
    gram = lax.dot_general(
        spectral, spectral, (((0,), (0,)), ((), ())), precision=lax.Precision.HIGHEST
    )
    gram = sum_over_devices(gram, core)
    lower_factor = jnp.linalg.cholesky(gram)
    solved = jax.scipy.linalg.solve_triangular(lower_factor, spectral.T, lower=True)
    node_total = embedding.shape[0] * NY * NZ * NC * NX
    return solved.T * jnp.sqrt(jnp.float32(node_total))


def solution(mesh):
    fine = Mesh(mesh.devices.reshape(NY, NZ, NC, NX), ("y", "z", "c", "x"))
    wide = ("y", "z", "c")
    placed = (
        P(("y", "z", "c", "x"), None),
        P(wide, "x", None, None, None),
        P(wide, "x", None),
        P(wide, "x", None),
        P(wide, "x"),
    )
    return jax.shard_map(
        local, mesh=fine, in_specs=placed, out_specs=P(("y", "z", "c", "x"), None), check_vma=False
    )
```

```python
import functools

import jax
import jax.numpy as jnp
import numpy as np
from jax import lax
from jax.experimental import pallas as pl
from jax.experimental.pallas import tpu as pltpu
from jax.sharding import Mesh, PartitionSpec as P

NY, NZ, NC, NX = 4, 8, 2, 4
PLANE = ("y", "z", "c")


def plane_index(y, z, c):
    return ((y % NY) * NZ + z % NZ) * NC + c


def step_pairs(hop):
    first = []
    for y in range(NY):
        for z in range(NZ):
            first.append((plane_index(y, z, 0), plane_index(y, z + hop, 0)))
            first.append((plane_index(y, z, 1), plane_index(y + hop, z, 1)))
    return first


def bundle_pairs(hop):
    second = []
    for y in range(NY):
        for z in range(NZ):
            second.append((plane_index(y, z, 0), plane_index(y + hop, z, 0)))
            second.append((plane_index(y, z, 1), plane_index(y, z + hop, 1)))
    return second


def axis_shift(value, axis, hop):
    n = lax.axis_size(axis)
    return lax.ppermute(value, axis, [(i, (i + hop) % n) for i in range(n)])


def axis_swap(value, axis, bit):
    n = lax.axis_size(axis)
    return lax.ppermute(value, axis, [(i, i ^ bit) for i in range(n)])


def stack_blocks(parts):
    which = lax.broadcasted_iota(jnp.int32, (len(parts), 1, 1), 0)
    shape = (len(parts),) + parts[0].shape
    out = jnp.broadcast_to(parts[-1][None], shape)
    for i in range(len(parts) - 2, -1, -1):
        out = jnp.where(which == i, parts[i][None], out)
    return out


def far_pairs():
    pairs = []
    for y in range(NY):
        for z in range(NZ):
            pairs.append((plane_index(y, z, 0), plane_index(y, z - 2, 0)))
            pairs.append((plane_index(y, z, 1), plane_index(y, z + 4, 1)))
    return pairs


def send(value, pairs):
    return lax.ppermute(value, PLANE, pairs)


def swap(value):
    return axis_shift(value, "c", 1)


def gather_blocks(block, core):
    zero = core == 0
    plus1, minus1, plus2 = step_pairs(1), step_pairs(-1), step_pairs(2)
    bplus, bminus = bundle_pairs(1), bundle_pairs(-1)
    a1 = send(block, plus1)
    a2 = send(block, minus1)
    a3 = send(block, plus2)
    a4 = send(block, far_pairs())
    lo = stack_blocks([block, a1, a2, a3])
    g1p = send(lo, bplus)
    g1m = send(lo, bminus)
    onward = jnp.where(zero, a3, a4)
    a5 = send(onward, plus1)
    a6 = send(a4, minus1)
    a7 = send(onward, plus2)
    hi = stack_blocks([a4, a5, a6, a7])
    g2p = send(g1p, bplus)
    second_minus, hi_kept = lax.optimization_barrier((jnp.where(zero, hi, g1m), hi))
    g2m = send(second_minus, bminus)
    g3p = send(jnp.where(zero, hi_kept, g2p), bplus)
    g3m = send(g2m, bminus)
    mine = [lo, hi_kept, g1p, g1m, g2p, g2m, g3p, g3m]
    theirs = [swap(v) for v in mine]
    return mine + theirs


def place_table():
    table = np.zeros((NC, NY, NZ), np.int32)
    lo_z, hi_z, col_y = [0, -1, 1, -2], [2, -3, 3, -4], [0, -1, 1, -2]
    rows = ((0, 0, lo_z), (1, 0, hi_z), (2, -1, lo_z), (3, 1, lo_z), (4, -2, lo_z), (5, 1, hi_z), (6, -1, hi_z), (7, 2, hi_z))
    columns = ((0, 0), (1, 4), (2, -1), (3, 1), (4, -2), (5, 2), (6, -3), (7, 3))
    for off in range(4):
        for piece, dy, offsets in rows:
            table[0, dy % NY, offsets[off] % NZ] = piece * 4 + off
        for piece, dz in columns:
            table[1, col_y[off] % NY, dz % NZ] = piece * 4 + off
    assert all(sorted(t.reshape(-1)) == list(range(NY * NZ)) for t in table)
    return table.reshape(-1)


def tile_kernel(rows, cols, counts, table, tiles, *refs):
    *pieces, own_ref, one_ref, two_ref, three_ref, acc, picked, held, sems = refs
    span = pieces[0].shape[0]
    slots = tiles.shape[0]
    live = counts[0]
    y, z, core, x = (lax.axis_index(a) for a in ("y", "z", "c", "x"))

    def place_of(s):
        col = cols[s]
        from_y, from_z, from_c = (col // (NZ * NC)) & (NY - 1), (col // NC) & (NZ - 1), col & (NC - 1)
        dy, dz = (from_y - y) & (NY - 1), (from_z - z) & (NZ - 1)
        place = table[(from_c * NY + dy) * NZ + dz]
        return place + jnp.where(from_c == core, 0, NY * NZ)

    def load(pair):
        return pltpu.make_async_copy(tiles.at[pl.ds(2 * pair, 2)], held.at[pl.ds(2 * pair, 2)], sems.at[pair])

    for pair in range(slots // 2):

        @pl.when(2 * pair < live)
        def _():
            load(pair).start()

    acc[...] = jnp.zeros_like(acc)

    def work(pair, carry):
        both = (2 * pair, 2 * pair + 1)
        for i, s in enumerate(both):
            place = place_of(s)
            for p, piece in enumerate(pieces):

                @pl.when(place // span == p)
                def _():
                    picked[i] = piece[place % span]

        load(pair).wait()
        products = [
            jnp.dot(held[s], picked[i], preferred_element_type=jnp.float32) for i, s in enumerate(both)
        ]
        for i, s in enumerate(both):
            row = jnp.where(s < live, (rows[s] - x) & (NX - 1), NX)
            acc[row] += products[i]
        return carry

    lax.fori_loop(0, (live + 1) // 2, work, 0)
    own_ref[...] = acc[0]
    one_ref[...] = acc[1].astype(jnp.bfloat16)
    two_ref[...] = acc[2].astype(jnp.bfloat16)
    three_ref[...] = acc[3].astype(jnp.bfloat16)


def apply_operator(block, tiles, lists, core):
    slots, tile, _ = tiles.shape
    assert slots % 2 == 0
    width = block.shape[1]
    pieces = gather_blocks(block, core)
    vmem = pl.BlockSpec(memory_space=pltpu.VMEM)
    shape = lambda t: jax.ShapeDtypeStruct((tile, width), t)
    own, one, two, three = pl.pallas_call(
        tile_kernel,
        out_shape=[shape(jnp.float32)] + [shape(jnp.bfloat16)] * 3,
        in_specs=[pl.BlockSpec(memory_space=pltpu.SMEM)] * 4 + [pl.BlockSpec(memory_space=pl.ANY)] + [vmem] * len(pieces),
        out_specs=[vmem] * 4,
        scratch_shapes=[
            pltpu.VMEM((NX + 1, tile, width), jnp.float32),
            pltpu.VMEM((2, tile, width), jnp.bfloat16),
            pltpu.VMEM((slots, tile, tile), jnp.bfloat16),
            pltpu.SemaphoreType.DMA((slots // 2,)),
        ],
        compiler_params=pltpu.CompilerParams(vmem_limit_bytes=40 << 20),
        cost_estimate=pl.CostEstimate(
            flops=2 * slots * tile * tile * width, bytes_accessed=slots * tile * (tile + width) * 2, transcendentals=0
        ),
        name="tile_products",
    )(*lists, tiles, *pieces)
    f32 = jnp.float32
    one = axis_shift(one, "x", 1)
    three = axis_shift(three, "x", 3)
    two = axis_shift(two, "x", 2)
    return own + one.astype(f32) + three.astype(f32) + two.astype(f32)


def sum_over_devices(gram):
    gram = gram + axis_swap(gram, "c", 1)
    for axis in ("x", "y"):
        gram = gram + axis_shift(gram, axis, 1) + axis_shift(gram, axis, 3) + axis_shift(gram, axis, 2)
    gram = gram + axis_shift(gram, "z", 2) + axis_shift(gram, "z", 6) + axis_shift(gram, "z", 4)
    return gram + axis_swap(gram, "z", 1)


STEP = 8


def finish_kernel(scale, gram_ref, spectral_ref, out_ref, work):
    n = gram_ref.shape[0]
    row_id = lax.broadcasted_iota(jnp.int32, (n, n), 0)
    col_id = lax.broadcasted_iota(jnp.int32, (n, n), 1)
    work[:, :n] = gram_ref[...]
    work[:, n:] = jnp.where(row_id == col_id, 1.0, 0.0)
    sub = lax.broadcasted_iota(jnp.int32, (STEP, n), 0)
    for k in range(n // STEP):
        lo = k * STEP
        left = work[lo : lo + STEP, :n]
        right = work[lo : lo + STEP, n:]
        columns = [jnp.broadcast_to(left[:, lo + j : lo + j + 1], (STEP, n)) for j in range(STEP)]
        for j in range(STEP):
            inv = lax.rsqrt(columns[j][j : j + 1, :])
            inv = inv * (1.5 - 0.5 * columns[j][j : j + 1, :] * inv * inv)
            row_l, row_r = left[j : j + 1, :] * inv, right[j : j + 1, :] * inv
            factor = jnp.where(sub > j, columns[j] * inv, 0.0)
            here = sub == j
            left = jnp.where(here, row_l, left - factor * row_l)
            right = jnp.where(here, row_r, right - factor * row_r)
            for i in range(j + 1, STEP):
                columns[i] = columns[i] - factor * (columns[i][j : j + 1, :] * inv)
        work[lo : lo + STEP, :n] = left
        work[lo : lo + STEP, n:] = right
        hi = lo + STEP
        if hi < n:
            panel = left[:, hi:]
            both = jnp.concatenate([left, right], axis=1)
            work[hi:, :] = work[hi:, :] - lax.dot_general(
                panel, both, (((0,), (0,)), ((), ())), precision=lax.Precision.HIGHEST,
                preferred_element_type=jnp.float32)
    out_ref[...] = lax.dot_general(
        spectral_ref[...], work[:, n:] * scale, (((1,), (1,)), ((), ())), precision=lax.Precision.HIGHEST,
        preferred_element_type=jnp.float32)


def finish(gram, spectral, scale):
    n = gram.shape[0]
    vmem = pl.BlockSpec(memory_space=pltpu.VMEM)
    return pl.pallas_call(functools.partial(finish_kernel, scale),
        out_shape=jax.ShapeDtypeStruct(spectral.shape, jnp.float32),
        in_specs=[vmem, vmem], out_specs=vmem,
        scratch_shapes=[pltpu.VMEM((n, 2*n), jnp.float32)], name="orthonormalize")(gram, spectral)


def local(embedding, tile_blocks, tile_row, tile_col, counts):
    tiles = tile_blocks.reshape(tile_blocks.shape[-3:])
    slots = tiles.shape[0]
    core = lax.axis_index("c")
    lists = (tile_row.reshape(slots), tile_col.reshape(slots), counts.reshape(1), jnp.asarray(place_table()))

    def apply_once(_, carry):
        block, _, latest = carry
        applied = apply_operator(block, tiles, lists, core)
        return applied.astype(jnp.bfloat16), latest, applied

    start = (embedding.astype(jnp.bfloat16), jnp.zeros_like(embedding), embedding)
    _, first_order, applied = lax.fori_loop(0, 2, apply_once, start)
    second = 2.0 * applied - embedding
    spectral = 1.2661 * embedding - 1.1303 * first_order + 0.2715 * second
    gram = lax.dot_general(
        spectral, spectral, (((0,), (0,)), ((), ())), precision=lax.Precision.HIGHEST
    )
    node_total = embedding.shape[0] * NY * NZ * NC * NX
    return finish(sum_over_devices(gram), spectral, float(np.sqrt(node_total)))


def solution(mesh):
    fine = Mesh(mesh.devices.reshape(NY, NZ, NC, NX), ("y", "z", "c", "x"))
    wide = ("y", "z", "c")
    placed = (
        P(("y", "z", "c", "x"), None),
        P(wide, "x", None, None, None),
        P(wide, "x", None),
        P(wide, "x", None),
        P(wide, "x"),
    )
    return jax.shard_map(
        local, mesh=fine, in_specs=placed, out_specs=P(("y", "z", "c", "x"), None), check_vma=False
    )
```

```python
import functools

import jax
import jax.numpy as jnp
import numpy as np
from jax import lax
from jax.experimental import pallas as pl
from jax.experimental.pallas import tpu as pltpu
from jax.sharding import Mesh, PartitionSpec as P

NY, NZ, NC, NX = 4, 8, 2, 4
PLANE = ("y", "z", "c")


def plane_index(y, z, c):
    return ((y % NY) * NZ + z % NZ) * NC + c


def step_pairs(hop):
    first = []
    for y in range(NY):
        for z in range(NZ):
            first.append((plane_index(y, z, 0), plane_index(y, z + hop, 0)))
            first.append((plane_index(y, z, 1), plane_index(y + hop, z, 1)))
    return first


def bundle_pairs(hop):
    second = []
    for y in range(NY):
        for z in range(NZ):
            second.append((plane_index(y, z, 0), plane_index(y + hop, z, 0)))
            second.append((plane_index(y, z, 1), plane_index(y, z + hop, 1)))
    return second


def axis_shift(value, axis, hop):
    n = lax.axis_size(axis)
    return lax.ppermute(value, axis, [(i, (i + hop) % n) for i in range(n)])


def axis_swap(value, axis, bit):
    n = lax.axis_size(axis)
    return lax.ppermute(value, axis, [(i, i ^ bit) for i in range(n)])


def stack_blocks(parts):
    which = lax.broadcasted_iota(jnp.int32, (len(parts), 1, 1), 0)
    shape = (len(parts),) + parts[0].shape
    out = jnp.broadcast_to(parts[-1][None], shape)
    for i in range(len(parts) - 2, -1, -1):
        out = jnp.where(which == i, parts[i][None], out)
    return out


def far_pairs():
    pairs = []
    for y in range(NY):
        for z in range(NZ):
            pairs.append((plane_index(y, z, 0), plane_index(y, z - 2, 0)))
            pairs.append((plane_index(y, z, 1), plane_index(y, z + 4, 1)))
    return pairs


def send(value, pairs):
    return lax.ppermute(value, PLANE, pairs)


def swap(value):
    return axis_shift(value, "c", 1)


def gather_blocks(block, core):
    zero = core == 0
    plus1, minus1, plus2 = step_pairs(1), step_pairs(-1), step_pairs(2)
    bplus, bminus = bundle_pairs(1), bundle_pairs(-1)
    a1 = send(block, plus1)
    a2 = send(block, minus1)
    a3 = send(block, plus2)
    a4 = send(block, far_pairs())
    lo = stack_blocks([block, a1, a2, a3])
    g1p = send(lo, bplus)
    g1m = send(lo, bminus)
    onward = jnp.where(zero, a3, a4)
    a5 = send(onward, plus1)
    a6 = send(a4, minus1)
    a7 = send(onward, plus2)
    hi = stack_blocks([a4, a5, a6, a7])
    g2p = send(g1p, bplus)
    second_minus, hi_kept = lax.optimization_barrier((jnp.where(zero, hi, g1m), hi))
    g2m = send(second_minus, bminus)
    g3p = send(jnp.where(zero, hi_kept, g2p), bplus)
    g3m = send(g2m, bminus)
    mine = [lo, hi_kept, g1p, g1m, g2p, g2m, g3p, g3m]
    theirs = [swap(v) for v in mine]
    return mine + theirs


def place_table():
    table = np.zeros((NC, NY, NZ), np.int32)
    lo_z, hi_z, col_y = [0, -1, 1, -2], [2, -3, 3, -4], [0, -1, 1, -2]
    rows = ((0, 0, lo_z), (1, 0, hi_z), (2, -1, lo_z), (3, 1, lo_z), (4, -2, lo_z), (5, 1, hi_z), (6, -1, hi_z), (7, 2, hi_z))
    columns = ((0, 0), (1, 4), (2, -1), (3, 1), (4, -2), (5, 2), (6, -3), (7, 3))
    for off in range(4):
        for piece, dy, offsets in rows:
            table[0, dy % NY, offsets[off] % NZ] = piece * 4 + off
        for piece, dz in columns:
            table[1, col_y[off] % NY, dz % NZ] = piece * 4 + off
    assert all(sorted(t.reshape(-1)) == list(range(NY * NZ)) for t in table)
    return table.reshape(-1)


def tile_kernel(ids, final, rows, cols, counts, table, tiles, *refs):
    pieces, refs = refs[: len(ids)], refs[len(ids) :]
    if final:
        acc_in, own_ref, one_ref, two_ref, three_ref, acc, *refs = refs
    else:
        acc, *refs = refs
    picked, held, todo, sems = refs
    span = pieces[0].shape[0]
    live = counts[0]
    y, z, core, x = (lax.axis_index(a) for a in ("y", "z", "c", "x"))
    here = sum(1 << p for p in ids)

    def place_of(s):
        col = cols[s]
        from_y, from_z, from_c = (col // (NZ * NC)) & (NY - 1), (col // NC) & (NZ - 1), col & (NC - 1)
        dy, dz = (from_y - y) & (NY - 1), (from_z - z) & (NZ - 1)
        place = table[(from_c * NY + dy) * NZ + dz]
        return place + jnp.where(from_c == core, 0, NY * NZ)

    def load(s, k):
        return pltpu.make_async_copy(tiles.at[s], held.at[k], sems.at[k])

    def enlist(s, n):
        found = (here >> (place_of(s) // span)) & 1

        @pl.when(found == 1)
        def _():
            todo[n] = s
            load(s, n).start()

        return n + found

    total = lax.fori_loop(0, live, enlist, 0)
    if final:
        acc[:NX] = acc_in[:NX]
    else:
        acc[...] = jnp.zeros_like(acc)

    def pick(i, piece, offset, first, last):
        if last - first == 1:
            picked[i] = pieces[first][offset]
            return
        middle = (first + last) // 2

        @pl.when(piece < ids[middle])
        def _():
            pick(i, piece, offset, first, middle)

        @pl.when(piece >= ids[middle])
        def _():
            pick(i, piece, offset, middle, last)

    def work(pair, carry):
        targets, products = [], []
        for i in range(2):
            k = 2 * pair + i
            at = jnp.minimum(k, total - 1)
            s = todo[at]
            place = place_of(s)
            pick(i, place // span, place % span, 0, len(ids))

            @pl.when(k < total)
            def _():
                load(s, at).wait()

            targets.append((at, jnp.where(k < total, (rows[s] - x) & (NX - 1), NX)))
        for i in range(2):
            products.append(jnp.dot(held[targets[i][0]], picked[i], preferred_element_type=jnp.float32))
        for i in range(2):
            acc[targets[i][1]] += products[i]
        return carry

    lax.fori_loop(0, (total + 1) // 2, work, 0)
    if final:
        own_ref[...] = acc[0]
        one_ref[...] = acc[1].astype(jnp.bfloat16)
        two_ref[...] = acc[2].astype(jnp.bfloat16)
        three_ref[...] = acc[3].astype(jnp.bfloat16)


LATE = (6, 7, 14, 15)


def tile_products(pieces, tiles, lists):
    slots, tile, _ = tiles.shape
    width = pieces[0].shape[-1]
    early = tuple(p for p in range(len(pieces)) if p not in LATE)
    vmem = pl.BlockSpec(memory_space=pltpu.VMEM)
    shape = lambda t: jax.ShapeDtypeStruct((tile, width), t)
    sums = jax.ShapeDtypeStruct((NX + 1, tile, width), jnp.float32)
    scratch = [
        pltpu.VMEM((2, tile, width), jnp.bfloat16),
        pltpu.VMEM((slots, tile, tile), jnp.bfloat16),
        pltpu.SMEM((slots,), jnp.int32),
        pltpu.SemaphoreType.DMA((slots,)),
    ]

    def call(ids, final, out_shape, extra):
        share = len(ids) / len(pieces)
        return pl.pallas_call(
            functools.partial(tile_kernel, ids, final),
            out_shape=out_shape,
            in_specs=[pl.BlockSpec(memory_space=pltpu.SMEM)] * 4
            + [pl.BlockSpec(memory_space=pl.ANY)]
            + [vmem] * (len(ids) + len(extra)),
            out_specs=[vmem] * len(out_shape),
            scratch_shapes=([pltpu.VMEM(sums.shape, sums.dtype)] if final else []) + scratch,
            compiler_params=pltpu.CompilerParams(vmem_limit_bytes=40 << 20),
            cost_estimate=pl.CostEstimate(
                flops=int(share * 2 * slots * tile * tile * width),
                bytes_accessed=int(share * slots * tile * (tile + width) * 2),
                transcendentals=0,
            ),
        )(*lists, tiles, *(pieces[p] for p in ids), *extra)

    (partial,) = call(early, False, [sums], ())
    return call(LATE, True, [shape(jnp.float32)] + [shape(jnp.bfloat16)] * 3, (partial,))


def apply_operator(block, tiles, lists, core):
    own, one, two, three = tile_products(gather_blocks(block, core), tiles, lists)
    f32 = jnp.float32
    one = axis_shift(one, "x", 1)
    three = axis_shift(three, "x", 3)
    two = axis_shift(two, "x", 2)
    return own + one.astype(f32) + three.astype(f32) + two.astype(f32)


def sum_over_devices(gram):
    gram = gram + axis_swap(gram, "c", 1)
    for axis in ("x", "y"):
        gram = gram + axis_shift(gram, axis, 1) + axis_shift(gram, axis, 3) + axis_shift(gram, axis, 2)
    gram = gram + axis_shift(gram, "z", 2) + axis_shift(gram, "z", 6) + axis_shift(gram, "z", 4)
    return gram + axis_swap(gram, "z", 1)


STEP = 16


def finish_kernel(scale, gram_ref, spectral_ref, out_ref, work):
    step = STEP
    n = gram_ref.shape[0]
    work[...] = gram_ref[...]
    sub = lax.broadcasted_iota(jnp.int32, (step, n), 0)
    lane = lax.broadcasted_iota(jnp.int32, (step, n), 1)
    for k in range(n // step):
        lo = k * step
        hi = lo + step
        slab = work[lo:hi, :]
        columns = [jnp.broadcast_to(slab[:, lo + j : lo + j + 1], (step, n)) for j in range(step)]
        slab = jnp.where((lane >= lo) & (lane < hi), jnp.where(lane - lo == sub, 1.0, 0.0), slab)
        for j in range(step):
            pivot = columns[j][j : j + 1, :]
            inv = lax.rsqrt(pivot)
            inv = inv * (1.5 - 0.5 * pivot * inv * inv)
            row = slab[j : j + 1, :] * inv
            factor = jnp.where(sub > j, columns[j] * inv, 0.0)
            slab = jnp.where(sub == j, row, slab - factor * row)
            for i in range(j + 1, step):
                columns[i] = columns[i] - factor * (columns[i][j : j + 1, :] * inv)
        work[lo:hi, :] = slab
        if hi < n:
            rest = work[hi:, :]
            spot = lax.broadcasted_iota(jnp.int32, rest.shape, 1)
            rest = jnp.where((spot >= lo) & (spot < hi), 0.0, rest)
            work[hi:, :] = rest - lax.dot_general(
                slab[:, hi:], slab, (((0,), (0,)), ((), ())), precision=lax.Precision.HIGHEST,
                preferred_element_type=jnp.float32)
    upper = lax.broadcasted_iota(jnp.int32, (n, n), 1) > lax.broadcasted_iota(jnp.int32, (n, n), 0)
    inverse = jnp.where(upper, 0.0, work[...]) * scale
    out_ref[...] = lax.dot_general(
        spectral_ref[...], inverse, (((1,), (1,)), ((), ())), precision=lax.Precision.HIGHEST,
        preferred_element_type=jnp.float32)


def finish(gram, spectral, scale):
    n = gram.shape[0]
    vmem = pl.BlockSpec(memory_space=pltpu.VMEM)
    return pl.pallas_call(functools.partial(finish_kernel, scale),
        out_shape=jax.ShapeDtypeStruct(spectral.shape, jnp.float32),
        in_specs=[vmem, vmem], out_specs=vmem,
        scratch_shapes=[pltpu.VMEM((n, n), jnp.float32)], name="orthonormalize")(gram, spectral)


def local(embedding, tile_blocks, tile_row, tile_col, counts):
    tiles = tile_blocks.reshape(tile_blocks.shape[-3:])
    slots = tiles.shape[0]
    core = lax.axis_index("c")
    lists = (tile_row.reshape(slots), tile_col.reshape(slots), counts.reshape(1), jnp.asarray(place_table()))

    def apply_once(_, carry):
        block, _, latest = carry
        applied = apply_operator(block, tiles, lists, core)
        return applied.astype(jnp.bfloat16), latest, applied

    start = (embedding.astype(jnp.bfloat16), jnp.zeros_like(embedding), embedding)
    _, first_order, applied = lax.fori_loop(0, 2, apply_once, start)
    second = 2.0 * applied - embedding
    spectral = 1.2661 * embedding - 1.1303 * first_order + 0.2715 * second
    gram = lax.dot_general(
        spectral, spectral, (((0,), (0,)), ((), ())), precision=lax.Precision.HIGHEST
    )
    node_total = embedding.shape[0] * NY * NZ * NC * NX
    return finish(sum_over_devices(gram), spectral, float(np.sqrt(node_total)))


def solution(mesh):
    fine = Mesh(mesh.devices.reshape(NY, NZ, NC, NX), ("y", "z", "c", "x"))
    wide = ("y", "z", "c")
    placed = (
        P(("y", "z", "c", "x"), None),
        P(wide, "x", None, None, None),
        P(wide, "x", None),
        P(wide, "x", None),
        P(wide, "x"),
    )
    return jax.shard_map(
        local, mesh=fine, in_specs=placed, out_specs=P(("y", "z", "c", "x"), None), check_vma=False
    )
```

```python
import functools

import jax
import jax.numpy as jnp
import numpy as np
from jax import lax
from jax.experimental import pallas as pl
from jax.experimental.pallas import tpu as pltpu
from jax.sharding import Mesh, PartitionSpec as P

NY, NZ, NC, NX = 4, 8, 2, 4
PLANE = ("y", "z", "c")


def plane_index(y, z, c):
    return ((y % NY) * NZ + z % NZ) * NC + c


def moves(first, second):
    pairs = []
    for y in range(NY):
        for z in range(NZ):
            for c, (dy, dz) in enumerate((first, second)):
                pairs.append((plane_index(y, z, c), plane_index(y + dy, z + dz, c)))
    return pairs


def step_pairs(hop):
    return moves((0, hop), (hop, 0))


def bundle_pairs(hop):
    return moves((hop, 0), (0, hop))


def axis_shift(value, axis, hop):
    n = lax.axis_size(axis)
    return lax.ppermute(value, axis, [(i, (i + hop) % n) for i in range(n)])


def axis_swap(value, axis, bit):
    n = lax.axis_size(axis)
    return lax.ppermute(value, axis, [(i, i ^ bit) for i in range(n)])


def stack_blocks(parts):
    which = lax.broadcasted_iota(jnp.int32, (len(parts), 1, 1), 0)
    shape = (len(parts),) + parts[0].shape
    out = jnp.broadcast_to(parts[-1][None], shape)
    for i in range(len(parts) - 2, -1, -1):
        out = jnp.where(which == i, parts[i][None], out)
    return out


def send(value, pairs):
    return lax.ppermute(value, PLANE, pairs)


def swap(value):
    return axis_shift(value, "c", 1)


def gather_blocks(block, core):
    zero = core == 0
    plus, minus, plus_two = step_pairs(1), step_pairs(-1), step_pairs(2)
    bplus, bminus = bundle_pairs(1), bundle_pairs(-1)
    a3 = send(block, plus_two)
    a1 = send(block, plus)
    a2 = send(block, minus)
    a4 = send(block, moves((0, -2), (0, -2)))
    lo = stack_blocks([block, a1, a2, a3])
    g1p = send(lo, bplus)
    g1m = send(lo, bminus)
    a5 = send(jnp.where(zero, a3, a4), moves((0, 1), (0, -2)))
    a6 = send(jnp.where(zero, a4, a5), minus)
    a7 = send(jnp.where(zero, a3, a5), plus_two)
    a8 = send(a5, plus)
    rest = stack_blocks([a4, a5, a6, a7])
    g2p = send(g1p, bplus)
    second_minus, rest = lax.optimization_barrier((jnp.where(zero, rest, g1m), rest))
    g2m = send(second_minus, bminus)
    hi = jnp.where(zero, rest, stack_blocks([a5, a8, a6, a7]))
    g3p = send(jnp.where(zero, rest, g2p), bplus)
    g3m = send(g2m, bminus)
    mine = [lo, hi, g1p, g1m, g2p, g2m, g3p, g3m]
    return mine + [swap(v) for v in mine]


def place_table():
    table = np.zeros((NC, NY, NZ), np.int32)
    lo_z, hi_z, col_y = [0, -1, 1, -2], [2, -3, 3, -4], [0, -1, 1, -2]
    rows = ((0, 0, lo_z), (1, 0, hi_z), (2, -1, lo_z), (3, 1, lo_z), (4, -2, lo_z), (5, 1, hi_z), (6, -1, hi_z), (7, 2, hi_z))
    columns = ((0, 0), (1, 4), (2, -1), (3, 1), (4, -2), (5, 2), (6, -3), (7, 3))
    for off in range(4):
        for piece, dy, offsets in rows:
            table[0, dy % NY, offsets[off] % NZ] = piece * 4 + off
        for piece, dz in columns:
            table[1, col_y[off] % NY, dz % NZ] = piece * 4 + off
    assert all(sorted(t.reshape(-1)) == list(range(NY * NZ)) for t in table)
    return table.reshape(-1)


def tile_kernel(ids, final, rows, cols, counts, table, tiles, *refs):
    pieces, refs = refs[: len(ids)], refs[len(ids) :]
    if final:
        acc_in, own_ref, one_ref, two_ref, three_ref, acc, *refs = refs
    else:
        acc, *refs = refs
    picked, held, todo, sems = refs
    span = pieces[0].shape[0]
    live = counts[0]
    y, z, core, x = (lax.axis_index(a) for a in ("y", "z", "c", "x"))
    here = sum(1 << p for p in ids)

    def place_of(s):
        col = cols[s]
        from_y, from_z, from_c = (col // (NZ * NC)) & (NY - 1), (col // NC) & (NZ - 1), col & (NC - 1)
        dy, dz = (from_y - y) & (NY - 1), (from_z - z) & (NZ - 1)
        place = table[(from_c * NY + dy) * NZ + dz]
        return place + jnp.where(from_c == core, 0, NY * NZ)

    def load(s, k):
        return pltpu.make_async_copy(tiles.at[s], held.at[k], sems.at[k])

    def enlist(s, n):
        found = (here >> (place_of(s) // span)) & 1

        @pl.when(found == 1)
        def _():
            todo[n] = s
            load(s, n).start()

        return n + found

    total = lax.fori_loop(0, live, enlist, 0)
    if final:
        acc[:NX] = acc_in[:NX]
    else:
        acc[...] = jnp.zeros_like(acc)

    def pick(i, piece, offset, first, last):
        if last - first == 1:
            picked[i] = pieces[first][offset]
            return
        middle = (first + last) // 2

        @pl.when(piece < ids[middle])
        def _():
            pick(i, piece, offset, first, middle)

        @pl.when(piece >= ids[middle])
        def _():
            pick(i, piece, offset, middle, last)

    def work(pair, carry):
        targets, products = [], []
        for i in range(2):
            k = 2 * pair + i
            at = jnp.minimum(k, total - 1)
            s = todo[at]
            place = place_of(s)
            pick(i, place // span, place % span, 0, len(ids))

            @pl.when(k < total)
            def _():
                load(s, at).wait()

            targets.append((at, jnp.where(k < total, (rows[s] - x) & (NX - 1), NX)))
        for i in range(2):
            products.append(jnp.dot(held[targets[i][0]], picked[i], preferred_element_type=jnp.float32))
        for i in range(2):
            acc[targets[i][1]] += products[i]
        return carry

    lax.fori_loop(0, (total + 1) // 2, work, 0)
    if final:
        own_ref[...] = acc[0]
        one_ref[...] = acc[1].astype(jnp.bfloat16)
        two_ref[...] = acc[2].astype(jnp.bfloat16)
        three_ref[...] = acc[3].astype(jnp.bfloat16)


LATE = (6, 7, 14, 15)


def tile_products(pieces, tiles, lists):
    slots, tile, _ = tiles.shape
    width = pieces[0].shape[-1]
    early = tuple(p for p in range(len(pieces)) if p not in LATE)
    vmem = pl.BlockSpec(memory_space=pltpu.VMEM)
    shape = lambda t: jax.ShapeDtypeStruct((tile, width), t)
    sums = jax.ShapeDtypeStruct((NX + 1, tile, width), jnp.float32)
    scratch = [
        pltpu.VMEM((2, tile, width), jnp.bfloat16),
        pltpu.VMEM((slots, tile, tile), jnp.bfloat16),
        pltpu.SMEM((slots,), jnp.int32),
        pltpu.SemaphoreType.DMA((slots,)),
    ]

    def call(ids, final, out_shape, extra):
        share = len(ids) / len(pieces)
        return pl.pallas_call(
            functools.partial(tile_kernel, ids, final),
            out_shape=out_shape,
            in_specs=[pl.BlockSpec(memory_space=pltpu.SMEM)] * 4
            + [pl.BlockSpec(memory_space=pl.ANY)]
            + [vmem] * (len(ids) + len(extra)),
            out_specs=[vmem] * len(out_shape),
            scratch_shapes=([pltpu.VMEM(sums.shape, sums.dtype)] if final else []) + scratch,
            compiler_params=pltpu.CompilerParams(vmem_limit_bytes=40 << 20),
            cost_estimate=pl.CostEstimate(
                flops=int(share * 2 * slots * tile * tile * width),
                bytes_accessed=int(share * slots * tile * (tile + width) * 2),
                transcendentals=0,
            ),
        )(*lists, tiles, *(pieces[p] for p in ids), *extra)

    (partial,) = call(early, False, [sums], ())
    return call(LATE, True, [shape(jnp.float32)] + [shape(jnp.bfloat16)] * 3, (partial,))


def apply_operator(block, tiles, lists, core):
    own, one, two, three = tile_products(gather_blocks(block, core), tiles, lists)
    f32 = jnp.float32
    one = axis_shift(one, "x", 1)
    three = axis_shift(three, "x", 3)
    two = axis_shift(two, "x", 2)
    return own + one.astype(f32) + three.astype(f32) + two.astype(f32)


def sum_over_devices(gram):
    gram = gram + axis_swap(gram, "c", 1)
    for axis in ("x", "y"):
        gram = gram + axis_shift(gram, axis, 1) + axis_shift(gram, axis, 3) + axis_shift(gram, axis, 2)
    gram = gram + axis_shift(gram, "z", 2) + axis_shift(gram, "z", 6) + axis_shift(gram, "z", 4)
    return gram + axis_swap(gram, "z", 1)


STEP = 16


def finish_kernel(scale, gram_ref, spectral_ref, out_ref, work):
    step = STEP
    n = gram_ref.shape[0]
    work[...] = gram_ref[...]
    sub = lax.broadcasted_iota(jnp.int32, (step, n), 0)
    lane = lax.broadcasted_iota(jnp.int32, (step, n), 1)
    for k in range(n // step):
        lo = k * step
        hi = lo + step
        slab = work[lo:hi, :]
        columns = [jnp.broadcast_to(slab[:, lo + j : lo + j + 1], (step, n)) for j in range(step)]
        slab = jnp.where((lane >= lo) & (lane < hi), jnp.where(lane - lo == sub, 1.0, 0.0), slab)
        for j in range(step):
            pivot = columns[j][j : j + 1, :]
            inv = lax.rsqrt(pivot)
            inv = inv * (1.5 - 0.5 * pivot * inv * inv)
            row = slab[j : j + 1, :] * inv
            factor = jnp.where(sub > j, columns[j] * inv, 0.0)
            slab = jnp.where(sub == j, row, slab - factor * row)
            for i in range(j + 1, step):
                columns[i] = columns[i] - factor * (columns[i][j : j + 1, :] * inv)
        work[lo:hi, :] = slab
        if hi < n:
            rest = work[hi:, :]
            spot = lax.broadcasted_iota(jnp.int32, rest.shape, 1)
            rest = jnp.where((spot >= lo) & (spot < hi), 0.0, rest)
            work[hi:, :] = rest - lax.dot_general(
                slab[:, hi:], slab, (((0,), (0,)), ((), ())), precision=lax.Precision.HIGHEST,
                preferred_element_type=jnp.float32)
    upper = lax.broadcasted_iota(jnp.int32, (n, n), 1) > lax.broadcasted_iota(jnp.int32, (n, n), 0)
    inverse = jnp.where(upper, 0.0, work[...]) * scale
    out_ref[...] = lax.dot_general(
        spectral_ref[...], inverse, (((1,), (1,)), ((), ())), precision=lax.Precision.HIGHEST,
        preferred_element_type=jnp.float32)


def finish(gram, spectral, scale):
    n = gram.shape[0]
    vmem = pl.BlockSpec(memory_space=pltpu.VMEM)
    return pl.pallas_call(functools.partial(finish_kernel, scale),
        out_shape=jax.ShapeDtypeStruct(spectral.shape, jnp.float32),
        in_specs=[vmem, vmem], out_specs=vmem,
        scratch_shapes=[pltpu.VMEM((n, n), jnp.float32)], name="orthonormalize")(gram, spectral)


def local(embedding, tile_blocks, tile_row, tile_col, counts):
    tiles = tile_blocks.reshape(tile_blocks.shape[-3:])
    slots = tiles.shape[0]
    core = lax.axis_index("c")
    lists = (tile_row.reshape(slots), tile_col.reshape(slots), counts.reshape(1), jnp.asarray(place_table()))

    def apply_once(_, carry):
        block, _, latest = carry
        applied = apply_operator(block, tiles, lists, core)
        return applied.astype(jnp.bfloat16), latest, applied

    start = (embedding.astype(jnp.bfloat16), jnp.zeros_like(embedding), jnp.zeros_like(embedding))
    _, first_order, applied = lax.fori_loop(0, 2, apply_once, start)
    second = 2.0 * applied - embedding
    spectral = 1.2661 * embedding - 1.1303 * first_order + 0.2715 * second
    gram = lax.dot_general(
        spectral, spectral, (((0,), (0,)), ((), ())), precision=lax.Precision.HIGHEST
    )
    node_total = embedding.shape[0] * NY * NZ * NC * NX
    return finish(sum_over_devices(gram), spectral, float(np.sqrt(node_total)))


def solution(mesh):
    fine = Mesh(mesh.devices.reshape(NY, NZ, NC, NX), ("y", "z", "c", "x"))
    wide = ("y", "z", "c")
    placed = (
        P(("y", "z", "c", "x"), None),
        P(wide, "x", None, None, None),
        P(wide, "x", None),
        P(wide, "x", None),
        P(wide, "x"),
    )
    return jax.shard_map(
        local, mesh=fine, in_specs=placed, out_specs=P(("y", "z", "c", "x"), None), check_vma=False
    )
```

```python
import functools

import jax
import jax.numpy as jnp
import numpy as np
from jax import lax
from jax.experimental import pallas as pl
from jax.experimental.pallas import tpu as pltpu
from jax.sharding import Mesh, PartitionSpec as P

NY, NZ, NC, NX = 4, 8, 2, 4
PLANE = ("y", "z", "c")


def plane_index(y, z, c):
    return ((y % NY) * NZ + z % NZ) * NC + c


def step_pairs(hop):
    first = []
    for y in range(NY):
        for z in range(NZ):
            first.append((plane_index(y, z, 0), plane_index(y, z + hop, 0)))
            first.append((plane_index(y, z, 1), plane_index(y + hop, z, 1)))
    return first


def bundle_pairs(hop):
    second = []
    for y in range(NY):
        for z in range(NZ):
            second.append((plane_index(y, z, 0), plane_index(y + hop, z, 0)))
            second.append((plane_index(y, z, 1), plane_index(y, z + hop, 1)))
    return second


def side_pairs(hop):
    pairs = []
    for y in range(NY):
        for z in range(NZ):
            pairs.append((plane_index(y, z, 0), plane_index(y, z + hop, 0)))
            pairs.append((plane_index(y, z, 1), plane_index(y, z - hop, 1)))
    return pairs


def axis_shift(value, axis, hop):
    n = lax.axis_size(axis)
    return lax.ppermute(value, axis, [(i, (i + hop) % n) for i in range(n)])


def stack_blocks(parts):
    which = lax.broadcasted_iota(jnp.int32, (len(parts), 1, 1), 0)
    shape = (len(parts),) + parts[0].shape
    out = jnp.broadcast_to(parts[-1][None], shape)
    for i in range(len(parts) - 2, -1, -1):
        out = jnp.where(which == i, parts[i][None], out)
    return out


def far_pairs():
    pairs = []
    for y in range(NY):
        for z in range(NZ):
            pairs.append((plane_index(y, z, 0), plane_index(y, z - 2, 0)))
            pairs.append((plane_index(y, z, 1), plane_index(y, z + 4, 1)))
    return pairs


def send(value, pairs):
    return lax.ppermute(value, PLANE, pairs)


def swap(value):
    return axis_shift(value, "c", 1)


def gather_blocks(block, core):
    zero = core == 0
    plus1, minus1, plus2 = step_pairs(1), step_pairs(-1), step_pairs(2)
    bplus, bminus = bundle_pairs(1), bundle_pairs(-1)
    a1 = send(block, plus1)
    a2 = send(block, minus1)
    a3 = send(block, plus2)
    a4 = send(block, far_pairs())
    lo = stack_blocks([block, a1, a2, a3])
    g1p = send(lo, bplus)
    g1m = send(lo, bminus)
    onward = jnp.where(zero, a3, a4)
    a5 = send(onward, plus1)
    a6 = send(a4, minus1)
    a7 = send(onward, plus2)
    hi = stack_blocks([a4, a5, a6, a7])
    g2p = send(g1p, bplus)
    second_minus, hi_kept = lax.optimization_barrier((jnp.where(zero, hi, g1m), hi))
    g2m = send(second_minus, bminus)
    g3p = send(jnp.where(zero, hi_kept, g2p), bplus)
    g3m = send(g2m, bminus)
    mine = [lo, hi_kept, g1p, g1m, g2p, g2m, g3p, g3m]
    theirs = [swap(v) for v in mine]
    return mine + theirs


def place_table():
    table = np.zeros((NC, NY, NZ), np.int32)
    lo_z, hi_z, col_y = [0, -1, 1, -2], [2, -3, 3, -4], [0, -1, 1, -2]
    rows = ((0, 0, lo_z), (1, 0, hi_z), (2, -1, lo_z), (3, 1, lo_z), (4, -2, lo_z), (5, 1, hi_z), (6, -1, hi_z), (7, 2, hi_z))
    columns = ((0, 0), (1, 4), (2, -1), (3, 1), (4, -2), (5, 2), (6, -3), (7, 3))
    for off in range(4):
        for piece, dy, offsets in rows:
            table[0, dy % NY, offsets[off] % NZ] = piece * 4 + off
        for piece, dz in columns:
            table[1, col_y[off] % NY, dz % NZ] = piece * 4 + off
    assert all(sorted(t.reshape(-1)) == list(range(NY * NZ)) for t in table)
    return table.reshape(-1)


def tile_kernel(ids, final, rows, cols, counts, table, tiles, *refs):
    pieces, refs = refs[: len(ids)], refs[len(ids) :]
    if final:
        acc_in, own_ref, one_ref, two_ref, three_ref, acc, *refs = refs
    else:
        acc, *refs = refs
    picked, held, todo, sems = refs
    span = pieces[0].shape[0]
    live = counts[0]
    y, z, core, x = (lax.axis_index(a) for a in ("y", "z", "c", "x"))
    here = sum(1 << p for p in ids)

    def place_of(s):
        col = cols[s]
        from_y, from_z, from_c = (col // (NZ * NC)) & (NY - 1), (col // NC) & (NZ - 1), col & (NC - 1)
        dy, dz = (from_y - y) & (NY - 1), (from_z - z) & (NZ - 1)
        place = table[(from_c * NY + dy) * NZ + dz]
        return place + jnp.where(from_c == core, 0, NY * NZ)

    def load(s, k):
        return pltpu.make_async_copy(tiles.at[s], held.at[k], sems.at[k])

    def enlist(s, n):
        found = (here >> (place_of(s) // span)) & 1

        @pl.when(found == 1)
        def _():
            todo[n] = s
            load(s, n).start()

        return n + found

    total = lax.fori_loop(0, live, enlist, 0)
    if final:
        acc[:NX] = acc_in[:NX]
    else:
        acc[...] = jnp.zeros_like(acc)

    def pick(i, piece, offset, first, last):
        if last - first == 1:
            picked[i] = pieces[first][offset]
            return
        middle = (first + last) // 2

        @pl.when(piece < ids[middle])
        def _():
            pick(i, piece, offset, first, middle)

        @pl.when(piece >= ids[middle])
        def _():
            pick(i, piece, offset, middle, last)

    def work(pair, carry):
        targets, products = [], []
        for i in range(2):
            k = 2 * pair + i
            at = jnp.minimum(k, total - 1)
            s = todo[at]
            place = place_of(s)
            pick(i, place // span, place % span, 0, len(ids))

            @pl.when(k < total)
            def _():
                load(s, at).wait()

            targets.append((at, jnp.where(k < total, (rows[s] - x) & (NX - 1), NX)))
        for i in range(2):
            products.append(jnp.dot(held[targets[i][0]], picked[i], preferred_element_type=jnp.float32))
        for i in range(2):
            acc[targets[i][1]] += products[i]
        return carry

    lax.fori_loop(0, (total + 1) // 2, work, 0)
    if final:
        own_ref[...] = acc[0]
        one_ref[...] = acc[1].astype(jnp.bfloat16)
        two_ref[...] = acc[2].astype(jnp.bfloat16)
        three_ref[...] = acc[3].astype(jnp.bfloat16)


LATE = (6, 7, 14, 15)


def tile_products(pieces, tiles, lists):
    slots, tile, _ = tiles.shape
    width = pieces[0].shape[-1]
    early = tuple(p for p in range(len(pieces)) if p not in LATE)
    vmem = pl.BlockSpec(memory_space=pltpu.VMEM)
    shape = lambda t: jax.ShapeDtypeStruct((tile, width), t)
    sums = jax.ShapeDtypeStruct((NX + 1, tile, width), jnp.float32)
    scratch = [
        pltpu.VMEM((2, tile, width), jnp.bfloat16),
        pltpu.VMEM((slots, tile, tile), jnp.bfloat16),
        pltpu.SMEM((slots,), jnp.int32),
        pltpu.SemaphoreType.DMA((slots,)),
    ]

    def call(ids, final, out_shape, extra):
        share = len(ids) / len(pieces)
        return pl.pallas_call(
            functools.partial(tile_kernel, ids, final),
            out_shape=out_shape,
            in_specs=[pl.BlockSpec(memory_space=pltpu.SMEM)] * 4
            + [pl.BlockSpec(memory_space=pl.ANY)]
            + [vmem] * (len(ids) + len(extra)),
            out_specs=[vmem] * len(out_shape),
            scratch_shapes=([pltpu.VMEM(sums.shape, sums.dtype)] if final else []) + scratch,
            compiler_params=pltpu.CompilerParams(vmem_limit_bytes=(49 if final else 40) << 20),
            cost_estimate=pl.CostEstimate(
                flops=int(share * 2 * slots * tile * tile * width),
                bytes_accessed=int(share * slots * tile * (tile + width) * 2),
                transcendentals=0,
            ),
        )(*lists, tiles, *(pieces[p] for p in ids), *extra)

    (partial,) = call(early, False, [sums], ())
    return call(LATE, True, [shape(jnp.float32)] + [shape(jnp.bfloat16)] * 3, (partial,))


def apply_operator(block, tiles, lists, core):
    own, one, two, three = tile_products(gather_blocks(block, core), tiles, lists)
    f32 = jnp.float32
    one = axis_shift(one, "x", 1)
    three = axis_shift(three, "x", 3)
    two = axis_shift(two, "x", 2)
    return own + one.astype(f32) + three.astype(f32) + two.astype(f32)


def sum_over_devices(gram, core):
    gram = gram + axis_shift(gram, "c", 1)
    for axis in ("x", "y"):
        gram = gram + axis_shift(gram, axis, 1) + axis_shift(gram, axis, 3) + axis_shift(gram, axis, 2)
    zero = core == 0
    half = gram.shape[0] // 2
    side = [lax.ppermute(gram, PLANE, side_pairs(hop)) for hop in (1, 2, 3)]
    far = axis_shift(jnp.where(zero, gram[:half], gram[half:]), "z", 4)
    none = jnp.zeros_like(far)
    far = jnp.concatenate([jnp.where(zero, far, none), jnp.where(zero, none, far)], axis=0)
    part = side[0] + side[1] + side[2] + far
    return gram + (part + axis_shift(part, "c", 1))


STEP = 16


def finish_kernel(scale, gram_ref, spectral_ref, out_ref, work):
    step = STEP
    n = gram_ref.shape[0]
    work[...] = gram_ref[...]
    sub = lax.broadcasted_iota(jnp.int32, (step, n), 0)
    lane = lax.broadcasted_iota(jnp.int32, (step, n), 1)
    for k in range(n // step):
        lo = k * step
        hi = lo + step
        slab = work[lo:hi, :]
        columns = [jnp.broadcast_to(slab[:, lo + j : lo + j + 1], (step, n)) for j in range(step)]
        slab = jnp.where((lane >= lo) & (lane < hi), jnp.where(lane - lo == sub, 1.0, 0.0), slab)
        for j in range(step):
            pivot = columns[j][j : j + 1, :]
            inv = lax.rsqrt(pivot)
            inv = inv * (1.5 - 0.5 * pivot * inv * inv)
            row = slab[j : j + 1, :] * inv
            factor = jnp.where(sub > j, columns[j] * inv, 0.0)
            slab = jnp.where(sub == j, row, slab - factor * row)
            for i in range(j + 1, step):
                columns[i] = columns[i] - factor * (columns[i][j : j + 1, :] * inv)
        work[lo:hi, :] = slab
        if hi < n:
            rest = work[hi:, :]
            spot = lax.broadcasted_iota(jnp.int32, rest.shape, 1)
            rest = jnp.where((spot >= lo) & (spot < hi), 0.0, rest)
            work[hi:, :] = rest - lax.dot_general(
                slab[:, hi:], slab, (((0,), (0,)), ((), ())), precision=lax.Precision.HIGHEST,
                preferred_element_type=jnp.float32)
    upper = lax.broadcasted_iota(jnp.int32, (n, n), 1) > lax.broadcasted_iota(jnp.int32, (n, n), 0)
    inverse = jnp.where(upper, 0.0, work[...]) * scale
    out_ref[...] = lax.dot_general(
        spectral_ref[...], inverse, (((1,), (1,)), ((), ())), precision=lax.Precision.HIGHEST,
        preferred_element_type=jnp.float32)


def finish(gram, spectral, scale):
    n = gram.shape[0]
    vmem = pl.BlockSpec(memory_space=pltpu.VMEM)
    return pl.pallas_call(functools.partial(finish_kernel, scale),
        out_shape=jax.ShapeDtypeStruct(spectral.shape, jnp.float32),
        in_specs=[vmem, vmem], out_specs=vmem,
        scratch_shapes=[pltpu.VMEM((n, n), jnp.float32)], name="orthonormalize")(gram, spectral)


def local(embedding, tile_blocks, tile_row, tile_col, counts):
    tiles = tile_blocks.reshape(tile_blocks.shape[-3:])
    slots = tiles.shape[0]
    core = lax.axis_index("c")
    lists = (tile_row.reshape(slots), tile_col.reshape(slots), counts.reshape(1), jnp.asarray(place_table()))

    def apply_once(_, carry):
        block, _, latest = carry
        applied = apply_operator(block, tiles, lists, core)
        return applied.astype(jnp.bfloat16), latest, applied

    unread = 2.0 * embedding
    start = (embedding.astype(jnp.bfloat16), jnp.zeros_like(embedding), unread)
    _, first_order, applied = lax.fori_loop(0, 2, apply_once, start)
    second = 2.0 * applied - embedding
    spectral = 1.2661 * embedding - 1.1303 * first_order + 0.2715 * second
    gram = lax.dot_general(
        spectral, spectral, (((0,), (0,)), ((), ())), precision=lax.Precision.HIGHEST
    )
    node_total = embedding.shape[0] * NY * NZ * NC * NX
    return finish(sum_over_devices(gram, core), spectral, float(np.sqrt(node_total)))


def solution(mesh):
    fine = Mesh(mesh.devices.reshape(NY, NZ, NC, NX), ("y", "z", "c", "x"))
    wide = ("y", "z", "c")
    placed = (
        P(("y", "z", "c", "x"), None),
        P(wide, "x", None, None, None),
        P(wide, "x", None),
        P(wide, "x", None),
        P(wide, "x"),
    )
    return jax.shard_map(
        local, mesh=fine, in_specs=placed, out_specs=P(("y", "z", "c", "x"), None), check_vma=False
    )
```
